32 devices in a mesh: shard: 4 (over y, core), rep: 8 (over z, x).
Axes of the slice: x: 2, y: 2, z: 4, core: 2. Of those that a mesh axis runs over, the one named last changes fastest.
Arguments:
- tokens: bfloat16 [8192, 576], P(('shard', 'rep')), may hold values from -6 to 6
- cotangent: float32 [8192, 576], P(('shard', 'rep')), may hold values from -6 to 6
- starts: int32 [8192], P(('shard', 'rep')), may hold values from 0 to 1, as said below
- weights: float32 [1, 3543040], P(None, ('shard', 'rep')), may hold values from -2 to 2
- first_moment: float32 [1, 3543040], P(None, ('shard', 'rep')), may hold values from -6 to 6
- second_moment: float32 [1, 3543040], P(None, ('shard', 'rep')), may hold values from 32 to 128
Outputs:
- block_out: bfloat16 [8192, 576], P(('shard', 'rep'))
- input_grad: float32 [8192, 576], P(('shard', 'rep'))
- weight_grad: float32 [1, 3543040], P(None, ('shard', 'rep'))
- new_weights: float32 [1, 3543040], P(None, ('shard', 'rep'))
- new_first: float32 [1, 3543040], P(None, ('shard', 'rep'))
- new_second: float32 [1, 3543040], P(None, ('shard', 'rep'))
The draws below stay inside these ranges and needn't reach their ends.
Inputs may be any that keep to these rules, and one draw needn't show every extreme that they name: `starts`: each aligned micro-batch of 128 tokens begins with a 1; a sequence runs from a 1 to the token before the next 1 or the micro-batch's end; some micro-batch holds one sequence of 128 tokens.
All inputs are finite; a program needn't handle non-finite values.
Results may differ from the reference program's by a relative error of at most 0.022.
Values may be sent and summed in bfloat16 or wider, within the bound.
A program may use at most 128 MiB of HBM per device.

```python
import math
import jax
import jax.numpy as jnp
from jax import lax

D = 576
HEADS = 9
KV_HEADS = 3
HEAD_DIM = 64
FF = 1536
LAYERS = 1
MICRO = 2
STEP = 4
MB_CAP = 128
TOK_DEV = 256
TOKENS = 8192
PTOT = 3540096
NPAR = 3543040


def draw_starts(key, part):
    amount = TOKENS // MB_CAP
    key_level, key_bits, key_whole = jax.random.split(key, 3)
    level = jax.random.randint(key_level, (amount, 1), 1, 6)
    limit = jnp.left_shift(jnp.ones_like(level), 6 - level)
    raw_bits = jax.random.randint(key_bits, (amount, MB_CAP), 0, 64)
    flags = (raw_bits < limit).astype(jnp.int32)
    whole_idx = jax.random.randint(key_whole, (), 0, amount)
    single = jnp.arange(amount, dtype=jnp.int32)[:, None] == whole_idx
    flags = jnp.where(single, 0, flags)
    flags = flags.at[:, 0].set(1)
    return flags.reshape(TOKENS).astype(jnp.int32)


def draw_weights(key, part):
    q_width = HEADS * HEAD_DIM
    k_width = KV_HEADS * HEAD_DIM
    layer_rows = []
    for layer_idx in range(LAYERS):
        keys_all = jax.random.split(jax.random.fold_in(key, layer_idx), 12)

        def noise(slot, shape_one):
            return jnp.clip(jax.random.normal(keys_all[slot], shape_one, jnp.float32), -6.0, 6.0)
        attn_gain = 1.0 + 0.1 * noise(0, (D,))
        w_key = 0.5 * noise(2, (D, k_width)) / math.sqrt(D)
        w_query = 0.5 * noise(1, (D, q_width)) / math.sqrt(D)
        w_value = 1.25 * noise(3, (D, k_width)) / math.sqrt(D)
        w_out = noise(4, (q_width, D)) * 0.8 / math.sqrt(q_width)
        mlp_gain = 1.0 + 0.1 * noise(5, (D,))
        w_gate = noise(6, (D, FF)) / math.sqrt(D)
        w_up = noise(7, (D, FF)) / math.sqrt(D)
        w_down = noise(8, (FF, D)) / math.sqrt(FF)
        padding = 0.02 * noise(9, (NPAR - PTOT,))
        pieces = [attn_gain, w_query, w_key, w_value, w_out, mlp_gain, w_gate, w_up, w_down]
        layer_rows.append(jnp.concatenate([piece.reshape(-1) for piece in pieces] + [padding]))
    return jnp.clip(jnp.stack(layer_rows), -2.0, 2.0).astype(jnp.float32)


def steps_of(own_key, dims, cuts, smallest, largest):
    loudness = 1.0
    for position, shards_of in cuts:
        heights = jax.random.uniform(jax.random.fold_in(jax.random.fold_in(own_key, 6), position), (shards_of,), jnp.float32, smallest / len(cuts), largest / len(cuts))
        loudness = loudness * jnp.repeat(jnp.exp(heights), dims[position] // shards_of).reshape((-1,) + (1,) * (len(dims) - 1 - position))
    return loudness


def scatter_about(key, shape, spread, reach, cuts=(), kind=jnp.bfloat16):
    drawn = jax.random.normal(key, shape, jnp.float32) * spread
    if len(cuts) > 0:
        drawn = steps_of(key, shape, cuts, -0.22, 0.18) * drawn
    return jnp.clip(drawn, min=-reach, max=reach).astype(kind)


def setup_inputs(seed: int = 0) -> dict:
    key_of = jax.random.split(jax.random.key(seed), 7)
    return {
        "tokens": scatter_about(key_of[0], (TOKENS, D), 1.0, 6.0, ((0, 32),)),
        "cotangent": scatter_about(key_of[1], (TOKENS, D), 1.0, 6.0, ((0, 32),), jnp.float32),
        "starts": draw_starts(jax.random.fold_in(key_of[6], 71), 0),
        "weights": draw_weights(jax.random.fold_in(key_of[6], 71), 0),
        "first_moment": scatter_about(key_of[4], (LAYERS, NPAR), 1.0, 6.0, ((1, 32),), jnp.float32),
        "second_moment": jnp.clip(jnp.exp(math.log(128.0) - 1.3862944 * jax.random.uniform(key_of[5], (LAYERS, NPAR), jnp.float32) ** steps_of(key_of[5], (LAYERS, NPAR), ((1, 32),), -0.2, 0.2)), 32.0, 128.0),
    }


EPS_NORM = 1e-05
ROPE_BASE = 100000.0
MASK_FILL = -1e+30
BETA_ONE = 0.9
BETA_TWO = 0.95
RATE = 0.01
DECAY = 0.1
EPS_ADAM = 1e-08

def product(pattern, left_op, right_op):
    return jnp.einsum(pattern, left_op.astype(jnp.float32), right_op.astype(jnp.float32))

def unpack(flat_vec):
    q_width = HEADS * HEAD_DIM
    k_width = KV_HEADS * HEAD_DIM
    shapes = [(D,), (D, q_width), (D, k_width), (D, k_width), (q_width, D), (D,), (D, FF), (D, FF), (FF, D)]
    pieces = []
    offset = 0
    for shape_one in shapes:
        amount = math.prod(shape_one)
        pieces.append(flat_vec[offset:offset + amount].reshape(shape_one))
        offset = offset + amount
    return pieces

def pack_terms(grad_terms, padding):
    flat_parts = [term.reshape(-1) for term in grad_terms]
    return jnp.concatenate(flat_parts + [jnp.zeros((padding,), jnp.float32)])

def micro_setup(start_row):
    seq_id = jnp.cumsum(start_row).astype(jnp.int32)
    index_row = jnp.arange(start_row.shape[0], dtype=jnp.int32)
    allowed = (seq_id[:, None] == seq_id[None, :]) & (index_row[None, :] <= index_row[:, None])
    positions = (lax.optimization_barrier(jnp.sum(allowed.astype(jnp.int32), axis=1)) - 1).astype(jnp.int32)
    return (allowed, positions)

def rope_tables(positions):
    freq_idx = jnp.arange(HEAD_DIM // 2, dtype=jnp.float32)
    inverse = jnp.exp(-(2.0 * freq_idx / HEAD_DIM) * math.log(ROPE_BASE))
    angles = positions.astype(jnp.float32)[:, None] * inverse[None, :]
    angles = jnp.concatenate([angles, angles], axis=1)
    return (jnp.cos(angles)[:, None, :], jnp.sin(angles)[:, None, :])

def rotate(values, cos_table, sin_table):
    half_dim = values.shape[-1] // 2
    turned = jnp.concatenate([-values[..., half_dim:], values[..., :half_dim]], axis=-1)
    return values * cos_table + turned * sin_table

def unrotate(grads, cos_table, sin_table):
    half_dim = grads.shape[-1] // 2
    scaled = grads * sin_table
    turned = jnp.concatenate([scaled[..., half_dim:], -scaled[..., :half_dim]], axis=-1)
    return grads * cos_table + turned

def rms_scale(hidden):
    return lax.rsqrt(lax.optimization_barrier(jnp.mean(hidden * hidden, axis=-1, keepdims=True)) + EPS_NORM)

def norm_back(upstream, hidden, scale_rows, gain_f32):
    unit_rows = hidden * scale_rows
    weighted = upstream * gain_f32
    norm_grad = scale_rows * (weighted - unit_rows * lax.optimization_barrier(jnp.mean(weighted * unit_rows, axis=-1, keepdims=True)))
    return (norm_grad, lax.optimization_barrier(jnp.sum(upstream * unit_rows, axis=0)))

def masked_scores(grouped, key_vecs, allowed):
    scores = product('igrd,jgd->grij', grouped, key_vecs) * (1.0 / math.sqrt(HEAD_DIM))
    return jnp.where(allowed[None, None], scores, MASK_FILL)

def layer_forward(hidden, packed, allowed, cos_table, sin_table):
    attn_gain, w_query, w_key, w_value, w_out, mlp_gain, w_gate, w_up, w_down = packed
    row_count = hidden.shape[0]
    group_size = HEADS // KV_HEADS
    scale_one = rms_scale(hidden)
    normed_one = (hidden * scale_one * attn_gain.astype(jnp.float32)).astype(jnp.bfloat16)
    queries = rotate(product('rd,de->re', normed_one, w_query).reshape(row_count, HEADS, HEAD_DIM), cos_table, sin_table).astype(jnp.bfloat16)
    key_vecs = rotate(product('rd,de->re', normed_one, w_key).reshape(row_count, KV_HEADS, HEAD_DIM), cos_table, sin_table).astype(jnp.bfloat16)
    value_vecs = product('rd,de->re', normed_one, w_value).astype(jnp.bfloat16).reshape(row_count, KV_HEADS, HEAD_DIM)
    grouped = queries.reshape(row_count, KV_HEADS, group_size, HEAD_DIM)
    scores = masked_scores(grouped, key_vecs, allowed)
    row_top = lax.optimization_barrier(jnp.max(scores, axis=-1, keepdims=True))
    log_total = row_top + jnp.log(lax.optimization_barrier(jnp.sum(jnp.exp(scores - row_top), axis=-1, keepdims=True)))
    probs_b = jnp.exp(scores - log_total).astype(jnp.bfloat16)
    attended = product('grij,jgd->igrd', probs_b, value_vecs)
    att_flat = attended.astype(jnp.bfloat16).reshape(row_count, HEADS * HEAD_DIM)
    middle = hidden + product('re,ed->rd', att_flat, w_out)
    scale_two = rms_scale(middle)
    normed_two = (middle * scale_two * mlp_gain.astype(jnp.float32)).astype(jnp.bfloat16)
    gate_pre = product('rd,df->rf', normed_two, w_gate)
    up_pre = product('rd,df->rf', normed_two, w_up)
    activated = (jax.nn.silu(gate_pre) * up_pre).astype(jnp.bfloat16)
    result = middle + product('rf,fd->rd', activated, w_down)
    kept = (hidden, scale_one, normed_one, queries, key_vecs, value_vecs, log_total, attended, att_flat, middle, scale_two, normed_two, gate_pre, up_pre, activated)
    return (result, kept)

def layer_backward(upstream, packed, kept, allowed, cos_table, sin_table):
    attn_gain, w_query, w_key, w_value, w_out, mlp_gain, w_gate, w_up, w_down = packed
    hidden, scale_one, normed_one, queries, key_vecs, value_vecs, log_total, attended, att_flat, middle, scale_two, normed_two, gate_pre, up_pre, activated = kept
    row_count = hidden.shape[0]
    group_size = HEADS // KV_HEADS
    upstream_b = upstream.astype(jnp.bfloat16)
    g_down = product('rf,rd->fd', activated, upstream_b)
    d_act = product('rd,fd->rf', upstream_b, w_down)
    sigmoid_gate = jax.nn.sigmoid(gate_pre)
    d_gate = (d_act * up_pre * sigmoid_gate * (1.0 + gate_pre * (1.0 - sigmoid_gate))).astype(jnp.bfloat16)
    d_upper = (d_act * gate_pre * sigmoid_gate).astype(jnp.bfloat16)
    g_gate = product('rd,rf->df', normed_two, d_gate)
    g_up = product('rd,rf->df', normed_two, d_upper)
    d_norm_two = product('rf,df->rd', d_gate, w_gate) + product('rf,df->rd', d_upper, w_up)
    back_two, g_mlp_gain = norm_back(d_norm_two, middle, scale_two, mlp_gain.astype(jnp.float32))
    d_middle = upstream + back_two
    d_middle_b = d_middle.astype(jnp.bfloat16)
    g_out = product('re,rd->ed', att_flat, d_middle_b)
    d_att = product('rd,ed->re', d_middle_b, w_out).astype(jnp.bfloat16).reshape(row_count, KV_HEADS, group_size, HEAD_DIM)
    grouped = queries.reshape(row_count, KV_HEADS, group_size, HEAD_DIM)
    probs = jnp.exp(masked_scores(grouped, key_vecs, allowed) - log_total)
    probs_b = probs.astype(jnp.bfloat16)
    d_probs = product('igrd,jgd->grij', d_att, value_vecs)
    row_delta = jnp.transpose(lax.optimization_barrier(jnp.sum(d_att.astype(jnp.float32) * attended, axis=-1)), (1, 2, 0))[..., None]
    d_scores = (probs * (d_probs - row_delta) * (1.0 / math.sqrt(HEAD_DIM))).astype(jnp.bfloat16)
    d_values = product('grij,igrd->jgd', probs_b, d_att).astype(jnp.bfloat16)
    d_query = unrotate(product('grij,jgd->igrd', d_scores, key_vecs).reshape(row_count, HEADS, HEAD_DIM), cos_table, sin_table).astype(jnp.bfloat16)
    d_key = unrotate(product('grij,igrd->jgd', d_scores, grouped), cos_table, sin_table).astype(jnp.bfloat16)
    d_query = d_query.reshape(row_count, HEADS * HEAD_DIM)
    d_key = d_key.reshape(row_count, KV_HEADS * HEAD_DIM)
    d_values = d_values.reshape(row_count, KV_HEADS * HEAD_DIM)
    g_query = product('rd,re->de', normed_one, d_query)
    g_key = product('rd,re->de', normed_one, d_key)
    g_value = product('rd,re->de', normed_one, d_values)
    d_norm_one = product('re,de->rd', d_query, w_query) + product('re,de->rd', d_key, w_key) + product('re,de->rd', d_values, w_value)
    back_one, g_attn_gain = norm_back(d_norm_one, hidden, scale_one, attn_gain.astype(jnp.float32))
    grad_terms = [g_attn_gain, g_query, g_key, g_value, g_out, g_mlp_gain, g_gate, g_up, g_down]
    return (d_middle + back_one, grad_terms)

def reference(tokens, cotangent, starts, weights, first_moment, second_moment):
    compact = weights.astype(jnp.bfloat16)
    layers = [unpack(compact[layer_idx]) for layer_idx in range(LAYERS)]
    device_count = TOKENS // TOK_DEV

    def one_device(totals, inputs):
        dev_in, dev_cot, dev_start = inputs
        dev_terms = None
        out_list = []
        grad_list = []
        for micro_idx in range(MICRO):
            allowed, positions = micro_setup(dev_start[micro_idx])
            cos_table, sin_table = rope_tables(positions)
            hidden = dev_in[micro_idx].astype(jnp.float32)
            kept_all = []
            for layer_idx in range(LAYERS):
                hidden, kept = layer_forward(hidden, layers[layer_idx], allowed, cos_table, sin_table)
                kept_all.append(kept)
            out_list.append(hidden.astype(jnp.bfloat16))
            upstream = dev_cot[micro_idx].astype(jnp.float32)
            micro_terms = [None] * LAYERS
            for layer_idx in reversed(range(LAYERS)):
                upstream, grad_terms = layer_backward(upstream, layers[layer_idx], kept_all[layer_idx], allowed, cos_table, sin_table)
                micro_terms[layer_idx] = grad_terms
            grad_list.append(upstream)
            if dev_terms is None:
                dev_terms = micro_terms
            else:
                dev_terms = [[old + new for old, new in zip(dev_terms[layer_idx], micro_terms[layer_idx])] for layer_idx in range(LAYERS)]
        new_totals = []
        for layer_idx in range(LAYERS):
            rounded = [lax.optimization_barrier(term.astype(jnp.bfloat16)).astype(jnp.float32) for term in dev_terms[layer_idx]]
            new_totals.append([old + new for old, new in zip(totals[layer_idx], rounded)])
        return (new_totals, (jnp.stack(out_list), jnp.stack(grad_list)))
    initial = [[jnp.zeros(piece.shape, jnp.float32) for piece in layers[layer_idx]] for layer_idx in range(LAYERS)]
    totals, (out_all, grad_all) = lax.scan(one_device, initial, (tokens.reshape(device_count, MICRO, MB_CAP, D), cotangent.reshape(device_count, MICRO, MB_CAP, D), starts.reshape(device_count, MICRO, MB_CAP)))
    weight_grad = jnp.stack([pack_terms(totals[layer_idx], NPAR - PTOT) for layer_idx in range(LAYERS)])
    new_first = BETA_ONE * first_moment + (1.0 - BETA_ONE) * weight_grad
    new_second = BETA_TWO * second_moment + (1.0 - BETA_TWO) * weight_grad * weight_grad
    first_hat = new_first / (1.0 - BETA_ONE ** STEP)
    second_hat = new_second / (1.0 - BETA_TWO ** STEP)
    new_weights = weights - RATE * (first_hat / (jnp.sqrt(second_hat) + EPS_ADAM) + DECAY * weights)
    return (out_all.reshape(TOKENS, D), grad_all.reshape(TOKENS, D), weight_grad, new_weights, new_first, new_second)
```

```python
import functools
import math

import jax
import jax.numpy as jnp
from jax import lax
from jax.experimental import pallas as pl
from jax.experimental.pallas import tpu as pltpu
from jax.sharding import PartitionSpec as P

D = 576
HEADS = 9
KV_HEADS = 3
HEAD_DIM = 64
FF = 1536
MICRO = 2
STEP = 4
MB_CAP = 128
TOK = MICRO * MB_CAP
GROUP = HEADS // KV_HEADS
QW = 640
KW = 256
LANES = 128
BLK = 256

EPS_NORM = 1e-05
ROPE_BASE = 100000.0
MASK_FILL = -1e30
BETA_ONE = 0.9
BETA_TWO = 0.95
RATE = 0.01
DECAY = 0.1
EPS_ADAM = 1e-08

MESH = pl.DeviceIdType.MESH
F32 = jnp.float32
BF16 = jnp.bfloat16

U_QUERY = 9
U_KEY = U_QUERY + 9 * D
U_VALUE = U_KEY + 3 * D
U_OUT = U_VALUE + 3 * D
U_MLP_GAIN = U_OUT + 9 * D
ROW_GATE = (U_MLP_GAIN + 9) // 2
ROW_UP = ROW_GATE + 12 * D
ROW_DOWN = ROW_UP + 12 * D
U_DOWN = 2 * ROW_DOWN
ROW_END = ROW_DOWN + 9 * FF // 2


def grid_of(shard, rep):
    n = math.isqrt(rep // 2)
    deep = rep // n
    assert n * deep == rep and shard == 2 * n
    return n, deep


class Place:
    def __init__(self, n, deep):
        self.n, self.deep = n, deep
        shard, rep = lax.axis_index("shard"), lax.axis_index("rep")
        self.core = lax.rem(shard, 2)
        y = lax.div(shard, 2)
        self.z = lax.div(rep, n)
        x = lax.rem(rep, n)
        c = self.core
        self.a = x * (1 - c) + y * c
        self.b = y * (1 - c) + x * c

    def device(self, core, da, db, dz):
        c = self.core
        a, b, z = self.moved(self.a, da, self.n), self.moved(self.b, db, self.n), self.moved(self.z, dz, self.deep)
        x, y = a * (1 - c) + b * c, b * (1 - c) + a * c
        return (y * 2 + core, z * self.n + x)

    def moved(self, base, step, size):
        return lax.rem(base + (step + size), size) if step % size else base

    def piece(self, da, db, dz):
        shard, rep = self.device(self.core, da, db, dz)
        return shard * (self.n * self.deep) + rep

    def partner_piece(self, da, db, dz):
        shard, rep = self.device(1 - self.core, db, da, dz)
        return shard * (self.n * self.deep) + rep


def greet(devices):
    barrier = pltpu.get_barrier_semaphore()
    for device in devices:
        pl.semaphore_signal(barrier, inc=1, device_id=device, device_id_type=MESH)
    pl.semaphore_wait(barrier, len(devices))


def peers(place):
    n, deep = place.n, place.deep
    found = [place.device(1 - place.core, 0, 0, 0)]
    found += [place.device(place.core, 0, 0, d) for d in range(1, deep)]
    found += [place.device(place.core, d, 0, 0) for d in range(1, n)]
    found += [place.device(place.core, 0, d, 0) for d in range(1, n)]
    return found


def gather_kernel(n, deep, own_ref, out_ref, own_sem, zs, zr, xs, xr, ys, yr, ps, pr):
    place = Place(n, deep)
    greet(peers(place))
    core = place.core
    started = []

    def send(src, index, sems, recvs, slot, device):
        copy = pltpu.make_async_remote_copy(
            src_ref=src,
            dst_ref=out_ref.at[index],
            send_sem=sems.at[slot],
            recv_sem=recvs.at[slot],
            device_id=device,
            device_id_type=MESH,
        )
        copy.start()
        started.append(copy)
        return copy

    mine = place.piece(0, 0, 0)
    own_copy = pltpu.make_async_copy(own_ref, out_ref.at[mine], own_sem)
    own_copy.start()
    partner = place.device(1 - core, 0, 0, 0)
    arrive_z, arrive_a, arrive_b, arrive_p = {}, {}, {}, {}

    def spread_b(src, index, dz, da):
        for db in range(1, n):
            arrive_b[(dz, da, db)] = send(
                src, index, ys, yr, (dz * n + da) * (n - 1) + db - 1,
                place.device(core, 0, db, 0),
            )

    def spread_p(src, index, dz, da, db):
        arrive_p[(dz, da, db)] = send(src, index, ps, pr, (dz * n + da) * n + db, partner)

    def spread_a(src, index, dz):
        for da in range(1, n):
            arrive_a[(dz, da)] = send(
                src, index, xs, xr, dz * (n - 1) + da - 1, place.device(core, da, 0, 0)
            )

    for dz in range(1, deep):
        arrive_z[dz] = send(own_ref, mine, zs, zr, dz - 1, place.device(core, 0, 0, dz))
    spread_a(own_ref, mine, 0)
    spread_b(own_ref, mine, 0, 0)
    spread_p(own_ref, mine, 0, 0, 0)
    for dz in range(deep):
        if dz:
            arrive_z[dz].wait_recv()
            index = place.piece(0, 0, -dz)
            spread_a(out_ref.at[index], index, dz)
            spread_b(out_ref.at[index], index, dz, 0)
            spread_p(out_ref.at[index], index, dz, 0, 0)
        if dz >= 1:
            relay_a(place, out_ref, arrive_a, spread_b, spread_p, dz - 1, n)
    relay_a(place, out_ref, arrive_a, spread_b, spread_p, deep - 1, n)
    for dz in range(deep):
        for da in range(n):
            for db in range(1, n):
                arrive_b[(dz, da, db)].wait_recv()
                index = place.piece(-da, -db, -dz)
                spread_p(out_ref.at[index], index, dz, da, db)
    own_copy.wait()
    for copy in arrive_p.values():
        copy.wait_recv()
    for copy in started:
        copy.wait_send()


def relay_a(place, out_ref, arrive_a, spread_b, spread_p, dz, n):
    for da in range(1, n):
        arrive_a[(dz, da)].wait_recv()
        index = place.piece(-da, 0, -dz)
        spread_b(out_ref.at[index], index, dz, da)
        spread_p(out_ref.at[index], index, dz, da, 0)


def gather(own, n, deep):
    pieces = 2 * n * n * deep
    rows = own.shape[0]
    dma = pltpu.SemaphoreType.DMA
    return pl.pallas_call(
        functools.partial(gather_kernel, n, deep),
        out_shape=jax.ShapeDtypeStruct((pieces, rows, LANES), BF16),
        in_specs=[pl.BlockSpec(memory_space=pltpu.VMEM)],
        out_specs=pl.BlockSpec(memory_space=pl.ANY),
        scratch_shapes=[
            dma,
            dma((deep - 1,)), dma((deep - 1,)),
            dma((deep * (n - 1),)), dma((deep * (n - 1),)),
            dma((deep * n * (n - 1),)), dma((deep * n * (n - 1),)),
            dma((deep * n * n,)), dma((deep * n * n,)),
        ],
        compiler_params=pltpu.CompilerParams(collective_id=0, has_side_effects=True),
        name="gather_pieces",
    )(own)


def scatter_kernel(
    n, deep, rows, full_ref, sum_ref, got_p, held, got_b, got_a, got_z,
    ps, pr, bs, br, as_, ar, zs, zr,
):
    place = Place(n, deep)
    greet(peers(place))
    core = place.core
    started = []

    def send(src, dst, sems, recvs, slot, device):
        copy = pltpu.make_async_remote_copy(
            src_ref=src,
            dst_ref=dst.at[slot],
            send_sem=sems.at[slot],
            recv_sem=recvs.at[slot],
            device_id=device,
            device_id_type=MESH,
        )
        copy.start()
        started.append(copy)
        return copy

    partner = place.device(1 - core, 0, 0, 0)
    z_order = list(range(1, deep)) + [0]
    a_order = list(range(1, n)) + [0]
    b_order = list(range(1, n)) + [0]
    slot_p = lambda dz, da, db: (dz * n + da) * n + db
    slot_b = lambda dz, da, db: (dz * n + da) * (n - 1) + db - 1
    slot_a = lambda dz, da: dz * (n - 1) + da - 1
    order = [(dz, da, db) for db in b_order for dz in z_order for da in a_order]
    in_p, in_b, in_a, in_z = {}, {}, {}, {}
    for dz, da, db in order:
        in_p[(dz, da, db)] = send(
            full_ref.at[place.partner_piece(da, db, dz)], got_p, ps, pr, slot_p(dz, da, db), partner
        )
    for dz, da, db in order:
        in_p[(dz, da, db)].wait_recv()
        slot = slot_p(dz, da, db)
        here = full_ref[place.piece(da, db, dz)].astype(F32)
        held[slot] = (here + got_p[slot].astype(F32)).astype(BF16)
        if db:
            in_b[(dz, da, db)] = send(
                held.at[slot], got_b, bs, br, slot_b(dz, da, db), place.device(core, 0, db, 0)
            )
    for dz in z_order:
        for da in a_order:
            slot = slot_p(dz, da, 0)
            total = held[slot].astype(F32)
            for db in range(1, n):
                in_b[(dz, da, db)].wait_recv()
                total = total + got_b[slot_b(dz, da, db)].astype(F32)
            held[slot] = total.astype(BF16)
            if da:
                in_a[(dz, da)] = send(
                    held.at[slot], got_a, as_, ar, slot_a(dz, da), place.device(core, da, 0, 0)
                )
    for dz in z_order:
        slot = slot_p(dz, 0, 0)
        total = held[slot].astype(F32)
        for da in range(1, n):
            in_a[(dz, da)].wait_recv()
            total = total + got_a[slot_a(dz, da)].astype(F32)
        if dz:
            held[slot] = total.astype(BF16)
            in_z[dz] = send(held.at[slot], got_z, zs, zr, dz - 1, place.device(core, 0, 0, dz))
        else:
            for step in range(1, deep):
                in_z[step].wait_recv()
                total = total + got_z[step - 1].astype(F32)
            sum_ref[...] = total
    for copy in started:
        copy.wait_send()


def scatter(packed, n, deep):
    rows = packed.shape[1]
    dma = pltpu.SemaphoreType.DMA
    cnt_p, cnt_b, cnt_a, cnt_z = deep * n * n, deep * n * (n - 1), deep * (n - 1), deep - 1
    slots = lambda amount: pltpu.VMEM((amount, rows, LANES), BF16)
    return pl.pallas_call(
        functools.partial(scatter_kernel, n, deep, rows),
        out_shape=jax.ShapeDtypeStruct((rows, LANES), F32),
        in_specs=[pl.BlockSpec(memory_space=pltpu.VMEM)],
        out_specs=pl.BlockSpec(memory_space=pltpu.VMEM),
        scratch_shapes=[
            slots(cnt_p), slots(cnt_p), slots(cnt_b), slots(cnt_a), slots(cnt_z),
            dma((cnt_p,)), dma((cnt_p,)), dma((cnt_b,)), dma((cnt_b,)),
            dma((cnt_a,)), dma((cnt_a,)), dma((cnt_z,)), dma((cnt_z,)),
        ],
        compiler_params=pltpu.CompilerParams(
            collective_id=1, has_side_effects=True, vmem_limit_bytes=48 << 20
        ),
        name="scatter_pieces",
    )(packed)


def mm(left, right):
    return lax.dot_general(left, right, (((1,), (0,)), ((), ())), preferred_element_type=F32)


def mm_nt(left, right):
    return lax.dot_general(left, right, (((1,), (1,)), ((), ())), preferred_element_type=F32)


def mm_tn(left, right):
    return lax.dot_general(left, right, (((0,), (0,)), ((), ())), preferred_element_type=F32)


def low_lanes(shape):
    return lax.broadcasted_iota(jnp.int32, shape, len(shape) - 1) < 64


def half_turn(values):
    return pltpu.roll(values, 64, 1)


def unpack_rows(flat, mid, dst, count, units, unit_offset):
    chunks = (units + 1) // 2
    half = count // 2
    low = low_lanes((half, LANES))
    for parity in range(2):
        first = unit_offset + parity * units
        base = first // 2
        for c in range(chunks):
            got = flat[pl.ds(base + c, half, stride=units), :]
            if first % 2:
                got = half_turn(got)
                if c < chunks - 1:
                    nxt = half_turn(flat[pl.ds(base + c + 1, half, stride=units), :])
                    got = jnp.where(low, got, nxt)
            if c == chunks - 1:
                got = jnp.where(low, got, 0.0)
            mid[c, pl.ds(parity, half, stride=2), :] = got
    for c in range(chunks):
        dst[:, c * LANES : (c + 1) * LANES] = mid[c, 0:count, :].astype(BF16)


def pack_rows(flat, mid, count, units, unit_offset):
    chunks = (units + 1) // 2
    half = count // 2
    low = low_lanes((half, LANES))
    for parity in range(2):
        first = unit_offset + parity * units
        base = first // 2
        got = [mid[c, pl.ds(parity, half, stride=2), :] for c in range(chunks)]
        if first % 2:
            got = [half_turn(one) for one in got]
            place = pl.ds(base, half, stride=units)
            flat[place, :] = jnp.where(low, flat[place, :], got[0])
            for c in range(1, chunks):
                flat[pl.ds(base + c, half, stride=units), :] = jnp.where(low, got[c - 1], got[c])
        else:
            for c in range(chunks - 1):
                flat[pl.ds(base + c, half, stride=units), :] = got[c]
            place = pl.ds(base + chunks - 1, half, stride=units)
            flat[place, :] = jnp.where(low, got[-1], flat[place, :])


def gain_row(flat, unit_offset):
    low = low_lanes((1, LANES))
    base = unit_offset // 2
    rows = [flat[base + c : base + c + 1, :] for c in range(5)]
    if unit_offset % 2:
        rows = [half_turn(one) for one in rows]
        rows = [jnp.where(low, rows[c], rows[min(c + 1, 4)]) for c in range(5)]
    return jnp.concatenate(rows, axis=1)[:, :D]


def store_gain(flat, row_ref, unit_offset):
    low = low_lanes((1, LANES))
    base = unit_offset // 2
    got = [row_ref[0:1, c * LANES : (c + 1) * LANES] for c in range(5)]
    if unit_offset % 2:
        got = [half_turn(one) for one in got]
        flat[base : base + 1, :] = jnp.where(low, flat[base : base + 1, :], got[0])
        for c in range(1, 5):
            flat[base + c : base + c + 1, :] = jnp.where(low, got[c - 1], got[c])
    else:
        for c in range(4):
            flat[base + c : base + c + 1, :] = got[c]
        flat[base + 4 : base + 5, :] = jnp.where(low, got[4], flat[base + 4 : base + 5, :])


def turn(values, sign):
    width = values.shape[1]
    lane = lax.broadcasted_iota(jnp.int32, values.shape, 1)
    first = (lane & 63) < 32
    ahead = pltpu.roll(values, width - 32, 1)
    behind = pltpu.roll(values, 32, 1)
    return jnp.where(first, -ahead, behind) if sign > 0 else jnp.where(first, ahead, -behind)


def rms_scale(hidden):
    return lax.rsqrt(jnp.mean(hidden * hidden, axis=-1, keepdims=True) + EPS_NORM)


def norm_back(upstream, hidden, scale_rows, gain):
    unit_rows = hidden * scale_rows
    weighted = upstream * gain
    grad = scale_rows * (
        weighted - unit_rows * jnp.mean(weighted * unit_rows, axis=-1, keepdims=True)
    )
    return grad, jnp.sum(upstream * unit_rows, axis=0, keepdims=True)


def layer_kernel(
    pieces, rows, gath, tokens, cot, starts, out, igrad, packed,
    flat, mid, wq, wk, wv, wo, wg, wu, wd, q_s, k_s, v_s, p_s, o_s, ob_s, n2t_s, n2_s,
    gate_s, up_s, act_s, h2_s, acc_s, gb_s, dob_s, dq_s, dk_s, dv_s, row_s,
):
    for b in range(pieces):
        flat[b * rows : (b + 1) * rows, :] = gath[b].astype(F32)
    unpack_rows(flat, mid, wq, D, 9, U_QUERY)
    unpack_rows(flat, mid, wk, D, 3, U_KEY)
    unpack_rows(flat, mid, wv, D, 3, U_VALUE)
    unpack_rows(flat, mid, wo, D, 9, U_OUT)
    unpack_rows(flat, mid, wd, FF, 9, U_DOWN)
    for c in range(12):
        cols = slice(c * LANES, (c + 1) * LANES)
        wg[:, cols] = flat[pl.ds(ROW_GATE + c, D, stride=12), :].astype(BF16)
        wu[:, cols] = flat[pl.ds(ROW_UP + c, D, stride=12), :].astype(BF16)
    gain_one = gain_row(flat, 0)
    gain_two = gain_row(flat, U_MLP_GAIN)

    at_row = lax.broadcasted_iota(jnp.int32, (MB_CAP, MB_CAP), 0)
    at_col = lax.broadcasted_iota(jnp.int32, (MB_CAP, MB_CAP), 1)
    allowed, places = [], []
    for m in range(MICRO):
        flags = jnp.broadcast_to(starts[m : m + 1, :], (MB_CAP, MB_CAP))
        seen = jnp.where((flags > 0) & (at_col <= at_row), at_col, 0).astype(F32)
        begin = jnp.max(seen, axis=1, keepdims=True)
        here = (at_col <= at_row) & (at_col.astype(F32) >= begin)
        allowed.append(jnp.concatenate([here.astype(F32)] * GROUP, axis=0) > 0.0)
        places.append(at_row[:, 0:1].astype(F32) - begin)
    position = jnp.concatenate(places, axis=0)
    freq = (lax.broadcasted_iota(jnp.int32, (1, LANES), 1) & 31).astype(F32)
    inverse = jnp.exp(-(2.0 * freq / HEAD_DIM) * math.log(ROPE_BASE))
    angle = position * inverse
    cos_one, sin_one = jnp.cos(angle), jnp.sin(angle)
    cos_q, sin_q = jnp.concatenate([cos_one] * 5, axis=1), jnp.concatenate([sin_one] * 5, axis=1)
    cos_k, sin_k = cos_q[:, :KW], sin_q[:, :KW]

    hidden = tokens[...].astype(F32)
    scale_one = rms_scale(hidden)
    normed_one = (hidden * scale_one * gain_one).astype(BF16)
    query = mm(normed_one, wq[...])
    q_s[...] = (query * cos_q + turn(query, 1) * sin_q).astype(BF16)
    key = mm(normed_one, wk[...])
    k_s[...] = (key * cos_k + turn(key, 1) * sin_k).astype(BF16)
    v_s[...] = mm(normed_one, wv[...]).astype(BF16)

    def heads(ref, m, g):
        r = slice(m * MB_CAP, (m + 1) * MB_CAP)
        return jnp.concatenate(
            [ref[r, h * 64 : (h + 1) * 64] for h in range(g * GROUP, (g + 1) * GROUP)], axis=0
        )

    scale = 1.0 / math.sqrt(HEAD_DIM)
    for m in range(MICRO):
        r = slice(m * MB_CAP, (m + 1) * MB_CAP)
        for g in range(KV_HEADS):
            c = slice(g * 64, (g + 1) * 64)
            scores = mm_nt(heads(q_s, m, g), k_s[r, c]) * scale
            scores = jnp.where(allowed[m], scores, MASK_FILL)
            top = jnp.max(scores, axis=-1, keepdims=True)
            total = top + jnp.log(jnp.sum(jnp.exp(scores - top), axis=-1, keepdims=True))
            probs = jnp.exp(scores - total)
            slot = m * KV_HEADS + g
            p_s[slot] = probs
            attended = mm(probs.astype(BF16), v_s[r, c])
            o_s[slot] = attended
            for i in range(GROUP):
                h = g * GROUP + i
                ob_s[r, h * 64 : (h + 1) * 64] = attended[i * MB_CAP : (i + 1) * MB_CAP].astype(BF16)
    middle = hidden + mm(ob_s[...], wo[:, :D])
    h2_s[...] = middle
    scale_two = rms_scale(middle)
    normed_two = (middle * scale_two * gain_two).astype(BF16)
    n2_s[...] = normed_two
    n2t_s[...] = normed_two.T
    acc_s[...] = middle
    gb_s[...] = cot[...].astype(BF16)

    @pl.loop(0, FF // BLK)
    def _(j):
        cols = pl.ds(pl.multiple_of(j * BLK, BLK), BLK)
        gate = mm(n2_s[...], wg[:, cols])
        upper = mm(n2_s[...], wu[:, cols])
        act = (gate * jax.nn.sigmoid(gate) * upper).astype(BF16)
        gate_s[:, cols] = gate
        up_s[:, cols] = upper
        act_s[:, cols] = act
        acc_s[...] += mm(act, wd[cols, :D])

    out[...] = acc_s[...].astype(BF16)
    acc_s[...] = jnp.zeros_like(acc_s)

    @pl.loop(0, FF // BLK)
    def _(j):
        cols = pl.ds(pl.multiple_of(j * BLK, BLK), BLK)
        gb = gb_s[...]
        g_down = mm_tn(act_s[:, cols], gb)
        for c in range(4):
            mid[c, cols, :] = g_down[:, c * LANES : (c + 1) * LANES]
        mid[4, cols, 0:64] = g_down[:, 512:576]
        d_act = mm_nt(gb, wd[cols, :D])
        gate, upper = gate_s[:, cols], up_s[:, cols]
        sig = jax.nn.sigmoid(gate)
        d_gate = (d_act * upper * sig * (1.0 + gate * (1.0 - sig))).astype(BF16)
        d_up = (d_act * gate * sig).astype(BF16)
        g_gate = mm(n2t_s[...], d_gate)
        g_up = mm(n2t_s[...], d_up)
        for c in range(BLK // LANES):
            at = j * (BLK // LANES) + c
            flat[pl.ds(ROW_GATE + at, D, stride=12), :] = g_gate[:, c * LANES : (c + 1) * LANES]
            flat[pl.ds(ROW_UP + at, D, stride=12), :] = g_up[:, c * LANES : (c + 1) * LANES]
        acc_s[...] += mm_nt(d_gate, wg[:, cols]) + mm_nt(d_up, wu[:, cols])

    pack_rows(flat, mid, FF, 9, U_DOWN)

    def hold(grad, chunks):
        for c in range(chunks):
            width = min(LANES, grad.shape[1] - c * LANES)
            mid[c, 0:D, 0:width] = grad[:, c * LANES : c * LANES + width]

    middle = h2_s[...]
    back_two, g_gain_two = norm_back(acc_s[...], middle, scale_two, gain_two)
    row_s[0:1, 0:D] = g_gain_two
    store_gain(flat, row_s, U_MLP_GAIN)
    d_middle = cot[...] + back_two
    d_middle_b = d_middle.astype(BF16)
    acc_s[...] = d_middle
    hold(mm_tn(ob_s[...], d_middle_b), 5)
    pack_rows(flat, mid, D, 9, U_OUT)
    dob_s[...] = mm_nt(d_middle_b, wo[:, :D]).astype(BF16)
    dq_s[...] = jnp.zeros_like(dq_s)
    dk_s[...] = jnp.zeros_like(dk_s)
    dv_s[...] = jnp.zeros_like(dv_s)
    for m in range(MICRO):
        r = slice(m * MB_CAP, (m + 1) * MB_CAP)
        for g in range(KV_HEADS):
            c = slice(g * 64, (g + 1) * 64)
            slot = m * KV_HEADS + g
            d_o = heads(dob_s, m, g)
            probs = jnp.where(allowed[m], p_s[slot], 0.0)
            d_probs = mm_nt(d_o, v_s[r, c])
            delta = jnp.sum(d_o.astype(F32) * o_s[slot], axis=-1, keepdims=True)
            d_scores = (probs * (d_probs - delta) * scale).astype(BF16)
            dv_s[r, c] = mm_tn(probs.astype(BF16), d_o)
            d_q = mm(d_scores, k_s[r, c])
            for i in range(GROUP):
                h = g * GROUP + i
                dq_s[r, h * 64 : (h + 1) * 64] = d_q[i * MB_CAP : (i + 1) * MB_CAP]
            dk_s[r, c] = mm_tn(d_scores, heads(q_s, m, g))
    d_q = dq_s[...]
    d_q = (d_q * cos_q + turn(d_q * sin_q, -1)).astype(BF16)
    d_k = dk_s[...]
    d_k = (d_k * cos_k + turn(d_k * sin_k, -1)).astype(BF16)
    d_v = dv_s[...].astype(BF16)
    n1t = normed_one.T
    hold(mm(n1t, d_q), 5)
    pack_rows(flat, mid, D, 9, U_QUERY)
    hold(mm(n1t, d_k), 2)
    pack_rows(flat, mid, D, 3, U_KEY)
    hold(mm(n1t, d_v), 2)
    pack_rows(flat, mid, D, 3, U_VALUE)
    d_norm = mm_nt(d_q, wq[...]) + mm_nt(d_k, wk[...]) + mm_nt(d_v, wv[...])
    back_one, g_gain_one = norm_back(d_norm, hidden, scale_one, gain_one)
    row_s[0:1, 0:D] = g_gain_one
    store_gain(flat, row_s, 0)
    igrad[...] = acc_s[...] + back_one
    tail = pieces * rows - ROW_END
    flat[ROW_END : ROW_END + tail, :] = jnp.zeros((tail, LANES), F32)
    for b in range(pieces):
        packed[b] = flat[b * rows : (b + 1) * rows, :].astype(BF16)


def layer(gath, tokens, cot, starts):
    pieces, rows, _ = gath.shape
    vm = pltpu.VMEM
    spec = pl.BlockSpec(memory_space=pltpu.VMEM)
    return pl.pallas_call(
        functools.partial(layer_kernel, pieces, rows),
        out_shape=(
            jax.ShapeDtypeStruct((TOK, D), BF16),
            jax.ShapeDtypeStruct((TOK, D), F32),
            jax.ShapeDtypeStruct((pieces, rows, LANES), BF16),
        ),
        in_specs=[spec] * 4,
        out_specs=(spec,) * 3,
        scratch_shapes=[
            vm((pieces * rows, LANES), F32),
            vm((5, FF, LANES), F32),
            vm((D, QW), BF16), vm((D, KW), BF16), vm((D, KW), BF16), vm((D, QW), BF16),
            vm((D, FF), BF16), vm((D, FF), BF16), vm((FF, QW), BF16),
            vm((TOK, QW), BF16), vm((TOK, KW), BF16), vm((TOK, KW), BF16),
            vm((MICRO * KV_HEADS, GROUP * MB_CAP, MB_CAP), F32),
            vm((MICRO * KV_HEADS, GROUP * MB_CAP, HEAD_DIM), F32),
            vm((TOK, D), BF16), vm((D, TOK), BF16), vm((TOK, D), BF16),
            vm((TOK, FF), F32), vm((TOK, FF), F32), vm((TOK, FF), BF16),
            vm((TOK, D), F32), vm((TOK, D), F32), vm((TOK, D), BF16), vm((TOK, D), BF16),
            vm((TOK, QW), F32), vm((TOK, KW), F32), vm((TOK, KW), F32),
            vm((8, QW), F32),
        ],
        compiler_params=pltpu.CompilerParams(vmem_limit_bytes=62 << 20),
        name="layer_step",
    )(gath, tokens, cot, starts)


def per_device(n, deep, tokens, cotangent, starts, weights, first_moment, second_moment):
    length = weights.shape[1]
    rows = length // LANES
    own = weights.astype(BF16).reshape(rows, LANES)
    gath = gather(own, n, deep)
    block_out, input_grad, packed = layer(gath, tokens, cotangent, starts.reshape(MICRO, MB_CAP))
    shard_total = scatter(packed, n, deep).reshape(1, length)
    new_first = BETA_ONE * first_moment + (1.0 - BETA_ONE) * shard_total
    new_second = BETA_TWO * second_moment + (1.0 - BETA_TWO) * shard_total * shard_total
    first_hat = new_first / (1.0 - BETA_ONE**STEP)
    second_hat = new_second / (1.0 - BETA_TWO**STEP)
    new_weights = weights - RATE * (first_hat / (jnp.sqrt(second_hat) + EPS_ADAM) + DECAY * weights)
    return (block_out, input_grad, shard_total, new_weights, new_first, new_second)


def solution(mesh):
    n, deep = grid_of(mesh.shape["shard"], mesh.shape["rep"])
    tok, flat = P(("shard", "rep"), None), P(None, ("shard", "rep"))
    return jax.shard_map(
        functools.partial(per_device, n, deep),
        mesh=mesh,
        in_specs=(tok, tok, P(("shard", "rep")), flat, flat, flat),
        out_specs=(tok, tok, flat, flat, flat, flat),
        check_vma=False,
    )
```

```python
import functools
import math

import jax
import jax.numpy as jnp
from jax import lax
from jax.experimental import pallas as pl
from jax.experimental.pallas import tpu as pltpu
from jax.sharding import PartitionSpec as P

D = 576
HEADS = 9
KV_HEADS = 3
HEAD_DIM = 64
FF = 1536
MICRO = 2
STEP = 4
MB_CAP = 128
TOK = MICRO * MB_CAP
GROUP = HEADS // KV_HEADS
QW = 640
KW = 256
LANES = 128
BLK = 256

EPS_NORM = 1e-05
ROPE_BASE = 100000.0
MASK_FILL = -1e30
BETA_ONE = 0.9
BETA_TWO = 0.95
RATE = 0.01
DECAY = 0.1
EPS_ADAM = 1e-08

MESH = pl.DeviceIdType.MESH
F32 = jnp.float32
BF16 = jnp.bfloat16

U_QUERY = 9
U_KEY = U_QUERY + 9 * D
U_VALUE = U_KEY + 3 * D
U_OUT = U_VALUE + 3 * D
U_MLP_GAIN = U_OUT + 9 * D
ROW_GATE = (U_MLP_GAIN + 9) // 2
ROW_UP = ROW_GATE + 12 * D
ROW_DOWN = ROW_UP + 12 * D
U_DOWN = 2 * ROW_DOWN
ROW_END = ROW_DOWN + 9 * FF // 2


def grid_of(shard, rep):
    n = math.isqrt(rep // 2)
    deep = rep // n
    assert n * deep == rep and shard == 2 * n
    return n, deep


class Place:
    def __init__(self, n, deep):
        self.n, self.deep = n, deep
        shard, rep = lax.axis_index("shard"), lax.axis_index("rep")
        self.core = lax.rem(shard, 2)
        y = lax.div(shard, 2)
        self.z = lax.div(rep, n)
        x = lax.rem(rep, n)
        c = self.core
        self.a = x * (1 - c) + y * c
        self.b = y * (1 - c) + x * c

    def device(self, core, da, db, dz):
        c = self.core
        a, b, z = self.moved(self.a, da, self.n), self.moved(self.b, db, self.n), self.moved(self.z, dz, self.deep)
        x, y = a * (1 - c) + b * c, b * (1 - c) + a * c
        return (y * 2 + core, z * self.n + x)

    def moved(self, base, step, size):
        return lax.rem(base + (step + size), size) if step % size else base

    def piece_at(self, core, da, db, z):
        shard, rep = self.device(core, da, db, 0)
        return shard * (self.n * self.deep) + z * self.n + (rep - self.z * self.n)

    def piece(self, da, db, dz):
        shard, rep = self.device(self.core, da, db, dz)
        return shard * (self.n * self.deep) + rep

    def partner_piece(self, da, db, dz):
        shard, rep = self.device(1 - self.core, db, da, dz)
        return shard * (self.n * self.deep) + rep


def greet(devices):
    barrier = pltpu.get_barrier_semaphore()
    for device in devices:
        pl.semaphore_signal(barrier, inc=1, device_id=device, device_id_type=MESH)
    pl.semaphore_wait(barrier, len(devices))


def peers(place):
    n, deep = place.n, place.deep
    found = [place.device(1 - place.core, 0, 0, 0)]
    found += [place.device(place.core, 0, 0, d) for d in range(1, deep)]
    found += [place.device(place.core, d, 0, 0) for d in range(1, n)]
    found += [place.device(place.core, 0, d, 0) for d in range(1, n)]
    return found


def gather_kernel(n, deep, own_ref, out_ref, own_sem, us, ur, ds_, dr, xs, xr, ys, yr, ps, pr):
    place = Place(n, deep)
    greet(peers(place))
    core, z = place.core, place.z
    partner = place.device(1 - core, 0, 0, 0)
    mine = place.piece_at(core, 0, 0, z)

    def copy_of(src, index, sems, recvs, slot, device):
        return pltpu.make_async_remote_copy(
            src_ref=src,
            dst_ref=out_ref.at[index],
            send_sem=sems.at[slot],
            recv_sem=recvs.at[slot],
            device_id=device,
            device_id_type=MESH,
        )

    def landed(index, sems, recvs, slot):
        copy_of(own_ref, index, sems, recvs, slot, partner).wait_recv()

    def left(sems, recvs, slot):
        copy_of(own_ref, mine, sems, recvs, slot, partner).wait_send()

    own_copy = pltpu.make_async_copy(own_ref, out_ref.at[mine], own_sem)
    own_copy.start()

    slot_a = lambda zs, da: zs * (n - 1) + (da - 1)
    slot_b = lambda zs, da, db: (zs * n + da) * (n - 1) + (db - 1)
    slot_p = lambda zs, da, db: (zs * n + da) * n + db

    def spread_b(src, index, zs, da):
        for db in range(1, n):
            copy_of(src, index, ys, yr, slot_b(zs, da, db), place.device(core, 0, db, 0)).start()

    def spread_p(src, index, zs, da, db):
        copy_of(src, index, ps, pr, slot_p(zs, da, db), partner).start()

    def spread(src, index, zs):
        for da in range(1, n):
            copy_of(src, index, xs, xr, slot_a(zs, da), place.device(core, da, 0, 0)).start()
        spread_b(src, index, zs, 0)
        spread_p(src, index, zs, 0, 0)

    def relay_a(zs):
        for da in range(1, n):
            index = place.piece_at(core, -da, 0, zs)
            landed(index, xs, xr, slot_a(zs, da))
            spread_b(out_ref.at[index], index, zs, da)
            spread_p(out_ref.at[index], index, zs, da, 0)

    @pl.when(z + 1 < deep)
    def _():
        copy_of(own_ref, mine, us, ur, 0, place.device(core, 0, 0, 1)).start()

    @pl.when(z > 0)
    def _():
        copy_of(own_ref, mine, ds_, dr, 0, place.device(core, 0, 0, -1)).start()

    spread(own_ref, mine, z)
    for k in range(deep - 1):

        @pl.when(z - 1 - k >= 0)
        def _():
            zs = z - 1 - k
            index = place.piece_at(core, 0, 0, zs)
            landed(index, us, ur, k)
            if k + 1 < deep - 1:

                @pl.when(z + 1 < deep)
                def _():
                    copy_of(
                        out_ref.at[index], index, us, ur, k + 1, place.device(core, 0, 0, 1)
                    ).start()

            spread(out_ref.at[index], index, zs)

        @pl.when(z + 1 + k < deep)
        def _():
            zs = z + 1 + k
            index = place.piece_at(core, 0, 0, zs)
            landed(index, ds_, dr, k)
            if k + 1 < deep - 1:

                @pl.when(z > 0)
                def _():
                    copy_of(
                        out_ref.at[index], index, ds_, dr, k + 1, place.device(core, 0, 0, -1)
                    ).start()

            spread(out_ref.at[index], index, zs)

        if k == 0:
            relay_a(z)
        else:

            @pl.when(z - k >= 0)
            def _():
                relay_a(z - k)

            @pl.when(z + k < deep)
            def _():
                relay_a(z + k)

    @pl.when(z - (deep - 1) >= 0)
    def _():
        relay_a(z - (deep - 1))

    @pl.when(z + (deep - 1) < deep)
    def _():
        relay_a(z + (deep - 1))

    way = 1 - 2 * lax.div(z * 2, deep)
    for step in range(deep):
        zs = lax.rem(z + way * step + deep, deep)
        for da in range(n):
            for db in range(1, n):
                index = place.piece_at(core, -da, -db, zs)
                landed(index, ys, yr, slot_b(zs, da, db))
                spread_p(out_ref.at[index], index, zs, da, db)
    own_copy.wait()
    for zs in range(deep):
        for da in range(n):
            for db in range(n):
                landed(place.piece_at(1 - core, -db, -da, zs), ps, pr, slot_p(zs, da, db))
                left(ps, pr, slot_p(zs, da, db))
                if db:
                    left(ys, yr, slot_b(zs, da, db))
            if da:
                left(xs, xr, slot_a(zs, da))
    for k in range(deep - 1):

        @pl.when((z + 1 < deep) & (k <= z))
        def _():
            left(us, ur, k)

        @pl.when((z > 0) & (k <= deep - 1 - z))
        def _():
            left(ds_, dr, k)


def gather(own, n, deep):
    pieces = 2 * n * n * deep
    rows = own.shape[0]
    dma = pltpu.SemaphoreType.DMA
    return pl.pallas_call(
        functools.partial(gather_kernel, n, deep),
        out_shape=jax.ShapeDtypeStruct((pieces, rows, LANES), BF16),
        in_specs=[pl.BlockSpec(memory_space=pltpu.VMEM)],
        out_specs=pl.BlockSpec(memory_space=pl.ANY),
        scratch_shapes=[
            dma,
            dma((deep - 1,)), dma((deep - 1,)), dma((deep - 1,)), dma((deep - 1,)),
            dma((deep * (n - 1),)), dma((deep * (n - 1),)),
            dma((deep * n * (n - 1),)), dma((deep * n * (n - 1),)),
            dma((deep * n * n,)), dma((deep * n * n,)),
        ],
        compiler_params=pltpu.CompilerParams(collective_id=0, has_side_effects=True),
        name="gather_pieces",
    )(own)


def scatter_kernel(
    n, deep, rows, full_ref, sum_ref, mine, got_p, held, got_b, got_a, got_z,
    ls, ps, pr, bs, br, as_, ar, zs, zr,
):
    place = Place(n, deep)
    greet(peers(place))
    core = place.core
    started = []

    def send(src, dst, sems, recvs, slot, device):
        copy = pltpu.make_async_remote_copy(
            src_ref=src,
            dst_ref=dst.at[slot],
            send_sem=sems.at[slot],
            recv_sem=recvs.at[slot],
            device_id=device,
            device_id_type=MESH,
        )
        copy.start()
        started.append(copy)
        return copy

    partner = place.device(1 - core, 0, 0, 0)
    z_order = list(range(1, deep)) + [0]
    a_order = list(range(1, n)) + [0]
    b_order = list(range(1, n)) + [0]
    slot_p = lambda dz, da, db: (dz * n + da) * n + db
    slot_b = lambda dz, da, db: (dz * n + da) * (n - 1) + db - 1
    slot_a = lambda dz, da: dz * (n - 1) + da - 1
    in_p, in_b, in_a, in_z, local = {}, {}, {}, {}, {}
    for dz in z_order:
        for db in b_order:
            for da in a_order:
                slot = slot_p(dz, da, db)
                in_p[(dz, da, db)] = send(
                    full_ref.at[place.partner_piece(da, db, dz)], got_p, ps, pr, slot, partner
                )
                local[slot] = pltpu.make_async_copy(
                    full_ref.at[place.piece(da, db, dz)], mine.at[slot], ls.at[slot]
                )
                local[slot].start()

    def stage_p(dz):
        for db in b_order:
            for da in a_order:
                slot = slot_p(dz, da, db)
                local[slot].wait()
                in_p[(dz, da, db)].wait_recv()
                held[slot] = (mine[slot].astype(F32) + got_p[slot].astype(F32)).astype(BF16)
                if db:
                    in_b[(dz, da, db)] = send(
                        held.at[slot], got_b, bs, br, slot_b(dz, da, db),
                        place.device(core, 0, db, 0),
                    )

    def stage_b(dz):
        for da in a_order:
            slot = slot_p(dz, da, 0)
            total = held[slot].astype(F32)
            for db in range(1, n):
                in_b[(dz, da, db)].wait_recv()
                total = total + got_b[slot_b(dz, da, db)].astype(F32)
            held[slot] = total.astype(BF16)
            if da:
                in_a[(dz, da)] = send(
                    held.at[slot], got_a, as_, ar, slot_a(dz, da), place.device(core, da, 0, 0)
                )

    def stage_a(dz):
        slot = slot_p(dz, 0, 0)
        total = held[slot].astype(F32)
        for da in range(1, n):
            in_a[(dz, da)].wait_recv()
            total = total + got_a[slot_a(dz, da)].astype(F32)
        if dz:
            held[slot] = total.astype(BF16)
            in_z[dz] = send(held.at[slot], got_z, zs, zr, dz - 1, place.device(core, 0, 0, dz))
        else:
            for step in range(1, deep):
                in_z[step].wait_recv()
                total = total + got_z[step - 1].astype(F32)
            sum_ref[...] = total

    for i in range(deep + 2):
        if i < deep:
            stage_p(z_order[i])
        if 0 <= i - 1 < deep:
            stage_b(z_order[i - 1])
        if 0 <= i - 2:
            stage_a(z_order[i - 2])
    for copy in started:
        copy.wait_send()


def scatter(packed, n, deep):
    rows = packed.shape[1]
    dma = pltpu.SemaphoreType.DMA
    cnt_p, cnt_b, cnt_a, cnt_z = deep * n * n, deep * n * (n - 1), deep * (n - 1), deep - 1
    slots = lambda amount: pltpu.VMEM((amount, rows, LANES), BF16)
    return pl.pallas_call(
        functools.partial(scatter_kernel, n, deep, rows),
        out_shape=jax.ShapeDtypeStruct((rows, LANES), F32),
        in_specs=[pl.BlockSpec(memory_space=pl.ANY)],
        out_specs=pl.BlockSpec(memory_space=pltpu.VMEM),
        scratch_shapes=[
            slots(cnt_p), slots(cnt_p), slots(cnt_p), slots(cnt_b), slots(cnt_a), slots(cnt_z),
            dma((cnt_p,)), dma((cnt_p,)), dma((cnt_p,)), dma((cnt_b,)), dma((cnt_b,)),
            dma((cnt_a,)), dma((cnt_a,)), dma((cnt_z,)), dma((cnt_z,)),
        ],
        compiler_params=pltpu.CompilerParams(
            collective_id=1, has_side_effects=True, vmem_limit_bytes=48 << 20
        ),
        name="scatter_pieces",
    )(packed)


def mm(left, right):
    return lax.dot_general(left, right, (((1,), (0,)), ((), ())), preferred_element_type=F32)


def mm_nt(left, right):
    return lax.dot_general(left, right, (((1,), (1,)), ((), ())), preferred_element_type=F32)


def mm_tn(left, right):
    return lax.dot_general(left, right, (((0,), (0,)), ((), ())), preferred_element_type=F32)


def low_lanes(shape):
    return lax.broadcasted_iota(jnp.int32, shape, len(shape) - 1) < 64


def half_turn(values):
    return pltpu.roll(values, 64, 1)


def unpack_rows(flat, mid, dst, count, units, unit_offset):
    chunks = (units + 1) // 2
    half = count // 2
    low = low_lanes((half, LANES))
    for parity in range(2):
        first = unit_offset + parity * units
        base = first // 2
        for c in range(chunks):
            got = flat[pl.ds(base + c, half, stride=units), :]
            if first % 2:
                got = half_turn(got)
                if c < chunks - 1:
                    nxt = half_turn(flat[pl.ds(base + c + 1, half, stride=units), :])
                    got = jnp.where(low, got, nxt)
            if c == chunks - 1:
                got = jnp.where(low, got, 0.0)
            mid[c, pl.ds(parity, half, stride=2), :] = got
    for c in range(chunks):
        dst[:, c * LANES : (c + 1) * LANES] = mid[c, 0:count, :].astype(BF16)


def pack_rows(flat, mid, count, units, unit_offset):
    chunks = (units + 1) // 2
    half = count // 2
    low = low_lanes((half, LANES))
    for parity in range(2):
        first = unit_offset + parity * units
        base = first // 2
        got = [mid[c, pl.ds(parity, half, stride=2), :] for c in range(chunks)]
        if first % 2:
            got = [half_turn(one) for one in got]
            place = pl.ds(base, half, stride=units)
            flat[place, :] = jnp.where(low, flat[place, :], got[0])
            for c in range(1, chunks):
                flat[pl.ds(base + c, half, stride=units), :] = jnp.where(low, got[c - 1], got[c])
        else:
            for c in range(chunks - 1):
                flat[pl.ds(base + c, half, stride=units), :] = got[c]
            place = pl.ds(base + chunks - 1, half, stride=units)
            flat[place, :] = jnp.where(low, got[-1], flat[place, :])


def gain_row(flat, unit_offset):
    low = low_lanes((1, LANES))
    base = unit_offset // 2
    rows = [flat[base + c : base + c + 1, :] for c in range(5)]
    if unit_offset % 2:
        rows = [half_turn(one) for one in rows]
        rows = [jnp.where(low, rows[c], rows[min(c + 1, 4)]) for c in range(5)]
    return jnp.concatenate(rows, axis=1)[:, :D]


def store_gain(flat, row_ref, unit_offset):
    low = low_lanes((1, LANES))
    base = unit_offset // 2
    got = [row_ref[0:1, c * LANES : (c + 1) * LANES] for c in range(5)]
    if unit_offset % 2:
        got = [half_turn(one) for one in got]
        flat[base : base + 1, :] = jnp.where(low, flat[base : base + 1, :], got[0])
        for c in range(1, 5):
            flat[base + c : base + c + 1, :] = jnp.where(low, got[c - 1], got[c])
    else:
        for c in range(4):
            flat[base + c : base + c + 1, :] = got[c]
        flat[base + 4 : base + 5, :] = jnp.where(low, got[4], flat[base + 4 : base + 5, :])


def turn(values, sign):
    width = values.shape[1]
    lane = lax.broadcasted_iota(jnp.int32, values.shape, 1)
    first = (lane & 63) < 32
    ahead = pltpu.roll(values, width - 32, 1)
    behind = pltpu.roll(values, 32, 1)
    return jnp.where(first, -ahead, behind) if sign > 0 else jnp.where(first, ahead, -behind)


def rms_scale(hidden):
    return lax.rsqrt(jnp.mean(hidden * hidden, axis=-1, keepdims=True) + EPS_NORM)


def norm_back(upstream, hidden, scale_rows, gain):
    unit_rows = hidden * scale_rows
    weighted = upstream * gain
    grad = scale_rows * (
        weighted - unit_rows * jnp.mean(weighted * unit_rows, axis=-1, keepdims=True)
    )
    return grad, jnp.sum(upstream * unit_rows, axis=0, keepdims=True)


def layer_kernel(
    pieces, rows, gath, tokens, cot, starts, out, igrad, packed,
    flat, mid, wq, wk, wv, wo, wg, wu, wd, q_s, k_s, v_s, p_s, o_s, ob_s, n2t_s, n2_s,
    gate_s, up_s, act_s, h2_s, acc_s, gb_s, dob_s, dq_s, dk_s, dv_s, row_s, cot_s,
):
    for b in range(pieces):
        flat[b * rows : (b + 1) * rows, :] = gath[b].astype(F32)
    unpack_rows(flat, mid, wq, D, 9, U_QUERY)
    unpack_rows(flat, mid, wk, D, 3, U_KEY)
    unpack_rows(flat, mid, wv, D, 3, U_VALUE)
    unpack_rows(flat, mid, wo, D, 9, U_OUT)
    unpack_rows(flat, mid, wd, FF, 9, U_DOWN)
    for c in range(12):
        cols = slice(c * LANES, (c + 1) * LANES)
        wg[:, cols] = flat[pl.ds(ROW_GATE + c, D, stride=12), :].astype(BF16)
        wu[:, cols] = flat[pl.ds(ROW_UP + c, D, stride=12), :].astype(BF16)
    gain_one = gain_row(flat, 0)
    gain_two = gain_row(flat, U_MLP_GAIN)

    at_row = lax.broadcasted_iota(jnp.int32, (MB_CAP, MB_CAP), 0)
    at_col = lax.broadcasted_iota(jnp.int32, (MB_CAP, MB_CAP), 1)
    allowed, places = [], []
    for m in range(MICRO):
        flags = jnp.broadcast_to(starts[m : m + 1, :], (MB_CAP, MB_CAP))
        seen = jnp.where((flags > 0) & (at_col <= at_row), at_col, 0).astype(F32)
        begin = jnp.max(seen, axis=1, keepdims=True)
        here = (at_col <= at_row) & (at_col.astype(F32) >= begin)
        allowed.append(jnp.concatenate([here.astype(F32)] * GROUP, axis=0) > 0.0)
        places.append(at_row[:, 0:1].astype(F32) - begin)
    position = jnp.concatenate(places, axis=0)
    freq = (lax.broadcasted_iota(jnp.int32, (1, LANES), 1) & 31).astype(F32)
    inverse = jnp.exp(-(2.0 * freq / HEAD_DIM) * math.log(ROPE_BASE))
    angle = position * inverse
    cos_one, sin_one = jnp.cos(angle), jnp.sin(angle)
    cos_q, sin_q = jnp.concatenate([cos_one] * 5, axis=1), jnp.concatenate([sin_one] * 5, axis=1)
    cos_k, sin_k = cos_q[:, :KW], sin_q[:, :KW]

    hidden = tokens[...].astype(F32).T
    scale_one = rms_scale(hidden)
    normed_one = (hidden * scale_one * gain_one).astype(BF16)
    query = mm(normed_one, wq[...])
    q_s[...] = (query * cos_q + turn(query, 1) * sin_q).astype(BF16)
    key = mm(normed_one, wk[...])
    k_s[...] = (key * cos_k + turn(key, 1) * sin_k).astype(BF16)
    v_s[...] = mm(normed_one, wv[...]).astype(BF16)

    def heads(ref, m, g):
        r = slice(m * MB_CAP, (m + 1) * MB_CAP)
        return jnp.concatenate(
            [ref[r, h * 64 : (h + 1) * 64] for h in range(g * GROUP, (g + 1) * GROUP)], axis=0
        )

    scale = 1.0 / math.sqrt(HEAD_DIM)
    for m in range(MICRO):
        r = slice(m * MB_CAP, (m + 1) * MB_CAP)
        for g in range(KV_HEADS):
            c = slice(g * 64, (g + 1) * 64)
            scores = mm_nt(heads(q_s, m, g), k_s[r, c]) * scale
            scores = jnp.where(allowed[m], scores, MASK_FILL)
            top = jnp.max(scores, axis=-1, keepdims=True)
            total = top + jnp.log(jnp.sum(jnp.exp(scores - top), axis=-1, keepdims=True))
            probs = jnp.exp(scores - total)
            slot = m * KV_HEADS + g
            p_s[slot] = probs
            attended = mm(probs.astype(BF16), v_s[r, c])
            o_s[slot] = attended
            for i in range(GROUP):
                h = g * GROUP + i
                ob_s[r, h * 64 : (h + 1) * 64] = attended[i * MB_CAP : (i + 1) * MB_CAP].astype(BF16)
    middle = hidden + mm(ob_s[...], wo[:, :D])
    h2_s[...] = middle
    scale_two = rms_scale(middle)
    normed_two = (middle * scale_two * gain_two).astype(BF16)
    n2_s[...] = normed_two
    n2t_s[...] = normed_two.T
    acc_s[...] = middle
    cot_s[...] = cot[...].T
    gb_s[...] = cot_s[...].astype(BF16)

    @pl.loop(0, FF // BLK)
    def _(j):
        cols = pl.ds(pl.multiple_of(j * BLK, BLK), BLK)
        gate = mm(n2_s[...], wg[:, cols])
        upper = mm(n2_s[...], wu[:, cols])
        act = (gate * jax.nn.sigmoid(gate) * upper).astype(BF16)
        gate_s[:, cols] = gate
        up_s[:, cols] = upper
        act_s[:, cols] = act
        acc_s[...] += mm(act, wd[cols, :D])

    out[...] = acc_s[...].T.astype(BF16)
    acc_s[...] = jnp.zeros_like(acc_s)

    @pl.loop(0, FF // BLK)
    def _(j):
        cols = pl.ds(pl.multiple_of(j * BLK, BLK), BLK)
        gb = gb_s[...]
        g_down = mm_tn(act_s[:, cols], gb)
        for c in range(4):
            mid[c, cols, :] = g_down[:, c * LANES : (c + 1) * LANES]
        mid[4, cols, 0:64] = g_down[:, 512:576]
        d_act = mm_nt(gb, wd[cols, :D])
        gate, upper = gate_s[:, cols], up_s[:, cols]
        sig = jax.nn.sigmoid(gate)
        d_gate = (d_act * upper * sig * (1.0 + gate * (1.0 - sig))).astype(BF16)
        d_up = (d_act * gate * sig).astype(BF16)
        g_gate = mm(n2t_s[...], d_gate)
        g_up = mm(n2t_s[...], d_up)
        for c in range(BLK // LANES):
            at = j * (BLK // LANES) + c
            flat[pl.ds(ROW_GATE + at, D, stride=12), :] = g_gate[:, c * LANES : (c + 1) * LANES]
            flat[pl.ds(ROW_UP + at, D, stride=12), :] = g_up[:, c * LANES : (c + 1) * LANES]
        acc_s[...] += mm_nt(d_gate, wg[:, cols]) + mm_nt(d_up, wu[:, cols])

    pack_rows(flat, mid, FF, 9, U_DOWN)

    def hold(grad, chunks):
        for c in range(chunks):
            width = min(LANES, grad.shape[1] - c * LANES)
            mid[c, 0:D, 0:width] = grad[:, c * LANES : c * LANES + width]

    middle = h2_s[...]
    back_two, g_gain_two = norm_back(acc_s[...], middle, scale_two, gain_two)
    row_s[0:1, 0:D] = g_gain_two
    store_gain(flat, row_s, U_MLP_GAIN)
    d_middle = cot_s[...] + back_two
    d_middle_b = d_middle.astype(BF16)
    acc_s[...] = d_middle
    hold(mm_tn(ob_s[...], d_middle_b), 5)
    pack_rows(flat, mid, D, 9, U_OUT)
    dob_s[...] = mm_nt(d_middle_b, wo[:, :D]).astype(BF16)
    dq_s[...] = jnp.zeros_like(dq_s)
    dk_s[...] = jnp.zeros_like(dk_s)
    dv_s[...] = jnp.zeros_like(dv_s)
    for m in range(MICRO):
        r = slice(m * MB_CAP, (m + 1) * MB_CAP)
        for g in range(KV_HEADS):
            c = slice(g * 64, (g + 1) * 64)
            slot = m * KV_HEADS + g
            d_o = heads(dob_s, m, g)
            probs = jnp.where(allowed[m], p_s[slot], 0.0)
            d_probs = mm_nt(d_o, v_s[r, c])
            delta = jnp.sum(d_o.astype(F32) * o_s[slot], axis=-1, keepdims=True)
            d_scores = (probs * (d_probs - delta) * scale).astype(BF16)
            dv_s[r, c] = mm_tn(probs.astype(BF16), d_o)
            d_q = mm(d_scores, k_s[r, c])
            for i in range(GROUP):
                h = g * GROUP + i
                dq_s[r, h * 64 : (h + 1) * 64] = d_q[i * MB_CAP : (i + 1) * MB_CAP]
            dk_s[r, c] = mm_tn(d_scores, heads(q_s, m, g))
    d_q = dq_s[...]
    d_q = (d_q * cos_q + turn(d_q * sin_q, -1)).astype(BF16)
    d_k = dk_s[...]
    d_k = (d_k * cos_k + turn(d_k * sin_k, -1)).astype(BF16)
    d_v = dv_s[...].astype(BF16)
    n1t = normed_one.T
    hold(mm(n1t, d_q), 5)
    pack_rows(flat, mid, D, 9, U_QUERY)
    hold(mm(n1t, d_k), 2)
    pack_rows(flat, mid, D, 3, U_KEY)
    hold(mm(n1t, d_v), 2)
    pack_rows(flat, mid, D, 3, U_VALUE)
    d_norm = mm_nt(d_q, wq[...]) + mm_nt(d_k, wk[...]) + mm_nt(d_v, wv[...])
    back_one, g_gain_one = norm_back(d_norm, hidden, scale_one, gain_one)
    row_s[0:1, 0:D] = g_gain_one
    store_gain(flat, row_s, 0)
    igrad[...] = (acc_s[...] + back_one).T
    tail = pieces * rows - ROW_END
    flat[ROW_END : ROW_END + tail, :] = jnp.zeros((tail, LANES), F32)
    for b in range(pieces):
        packed[b] = flat[b * rows : (b + 1) * rows, :].astype(BF16)


def layer(gath, tokens, cot, starts):
    pieces, rows, _ = gath.shape
    vm = pltpu.VMEM
    spec = pl.BlockSpec(memory_space=pltpu.VMEM)
    return pl.pallas_call(
        functools.partial(layer_kernel, pieces, rows),
        out_shape=(
            jax.ShapeDtypeStruct((D, TOK), BF16),
            jax.ShapeDtypeStruct((D, TOK), F32),
            jax.ShapeDtypeStruct((pieces, rows, LANES), BF16),
        ),
        in_specs=[spec] * 4,
        out_specs=(spec,) * 3,
        scratch_shapes=[
            vm((pieces * rows, LANES), F32),
            vm((5, FF, LANES), F32),
            vm((D, QW), BF16), vm((D, KW), BF16), vm((D, KW), BF16), vm((D, QW), BF16),
            vm((D, FF), BF16), vm((D, FF), BF16), vm((FF, QW), BF16),
            vm((TOK, QW), BF16), vm((TOK, KW), BF16), vm((TOK, KW), BF16),
            vm((MICRO * KV_HEADS, GROUP * MB_CAP, MB_CAP), F32),
            vm((MICRO * KV_HEADS, GROUP * MB_CAP, HEAD_DIM), F32),
            vm((TOK, D), BF16), vm((D, TOK), BF16), vm((TOK, D), BF16),
            vm((TOK, FF), F32), vm((TOK, FF), F32), vm((TOK, FF), BF16),
            vm((TOK, D), F32), vm((TOK, D), F32), vm((TOK, D), BF16), vm((TOK, D), BF16),
            vm((TOK, QW), F32), vm((TOK, KW), F32), vm((TOK, KW), F32),
            vm((8, QW), F32), vm((TOK, D), F32),
        ],
        compiler_params=pltpu.CompilerParams(vmem_limit_bytes=62 << 20),
        name="layer_step",
    )(gath, tokens, cot, starts)


def per_device(n, deep, tokens, cotangent, starts, weights, first_moment, second_moment):
    length = weights.shape[1]
    rows = length // LANES
    own = weights.astype(BF16).reshape(rows, LANES)
    gath = gather(own, n, deep)
    block_out, input_grad, packed = layer(
        gath, tokens.T, cotangent.T, starts.reshape(MICRO, MB_CAP)
    )
    shard_total = scatter(packed, n, deep).reshape(1, length)
    new_first = BETA_ONE * first_moment + (1.0 - BETA_ONE) * shard_total
    new_second = BETA_TWO * second_moment + (1.0 - BETA_TWO) * shard_total * shard_total
    first_hat = new_first / (1.0 - BETA_ONE**STEP)
    second_hat = new_second / (1.0 - BETA_TWO**STEP)
    new_weights = weights - RATE * (first_hat / (jnp.sqrt(second_hat) + EPS_ADAM) + DECAY * weights)
    return (block_out.T, input_grad.T, shard_total, new_weights, new_first, new_second)


def solution(mesh):
    n, deep = grid_of(mesh.shape["shard"], mesh.shape["rep"])
    tok, flat = P(("shard", "rep"), None), P(None, ("shard", "rep"))
    return jax.shard_map(
        functools.partial(per_device, n, deep),
        mesh=mesh,
        in_specs=(tok, tok, P(("shard", "rep")), flat, flat, flat),
        out_specs=(tok, tok, flat, flat, flat, flat),
        check_vma=False,
    )
```
